256 devices in a mesh: section: 8 (over y, core), expert: 32 (over x, z).
Axes of the slice: x: 4, y: 4, z: 8, core: 2. Of those that a mesh axis runs over, the one named last changes fastest.
Arguments:
- tokens_in: bfloat16 [8, 512, 2048], P(None, 'expert'), may hold values from -6 to 6
- expert_ids: int32 [8, 8, 512, 8], P('section'), may hold values from 0 to 31, as said below
- gate_values: float32 [8, 8, 512, 8], P('section', None, 'expert'), may hold values from 0.1 to 1
- expert_gate: bfloat16 [8, 32, 2048, 768], P('section', 'expert'), may hold values from -0.125 to 0.125
- expert_up: bfloat16 [8, 32, 2048, 768], P('section', 'expert'), may hold values from -0.125 to 0.125
- expert_down: bfloat16 [8, 32, 768, 2048], P('section', 'expert'), may hold values from -0.21875 to 0.21875
Outputs:
- layer_out: bfloat16 [8, 8, 512, 2048], P('section', None, 'expert')
The draws below stay inside these ranges and needn't reach their ends.
Inputs may be any that keep to these rules, and one draw needn't show every extreme that they name: `expert_ids`: every row names 8 different experts. In each layer and micro-batch the 16 rows of one device (aligned blocks) name no expert more than 6 times, and one expert is named exactly 6 times by the rows of every device.
All inputs are finite; a program needn't handle non-finite values.
Results may differ from the reference program's by a relative error of at most 0.025.
Values may be sent and summed in bfloat16 or wider, within the bound.
A program may use at most 64 MiB of HBM per device.

```python
import math
import jax
import jax.numpy as jnp
from jax import lax

D = 2048
FF = 768
TOPK = 8
TOK_DEV = 16
MB = 8
LAYERS = 8
EXPERT_TOTAL = 32
TOKENS = 512
MOST = 6
N_EXPERT = 32


def draw_expert_ids(key, part):
    base_key = jax.random.fold_in(key, 7)
    hot_key, shuffle_key, quota_key, row_key = jax.random.split(base_key, 4)
    blocks = LAYERS * MB * N_EXPERT
    hot_expert = jnp.repeat(jax.random.randint(hot_key, (LAYERS * MB,), 0, EXPERT_TOTAL), N_EXPERT)
    shuffle_keys = jax.random.split(shuffle_key, blocks)
    rank_values = jax.vmap(lambda sub_key: jax.random.permutation(sub_key, EXPERT_TOTAL))(shuffle_keys).astype(jnp.int32)
    labels = jnp.arange(EXPERT_TOTAL, dtype=jnp.int32)
    is_hot = labels[None, :] == hot_expert[:, None]
    scores = jnp.where(is_hot, -1, rank_values)
    label_order = jnp.argsort(scores, axis=1).astype(jnp.int32)
    total_other = TOK_DEV * TOPK - MOST
    default_allotment = total_other // (EXPERT_TOTAL - 1)
    leftover_count = total_other % (EXPERT_TOTAL - 1)
    spread = max(0, min(default_allotment, MOST - default_allotment - 1))
    extra_units = jax.random.randint(quota_key, (blocks, EXPERT_TOTAL - 1), 0, spread + 1)
    adjustment_slots = extra_units - jnp.roll(extra_units, 1, axis=1)
    surplus_slots = (jnp.arange(EXPERT_TOTAL - 1) < leftover_count).astype(jnp.int32)
    allotment_remaining = default_allotment + surplus_slots[None, :] + adjustment_slots
    quotas = jnp.concatenate([jnp.full((blocks, 1), MOST, jnp.int32), allotment_remaining.astype(jnp.int32)], axis=1)
    quota_ends = jnp.cumsum(quotas, axis=1)
    slot_order = jnp.arange(TOK_DEV * TOPK, dtype=jnp.int32)
    position = jnp.sum((quota_ends[:, None, :] <= slot_order[None, :, None]).astype(jnp.int32), axis=2)
    chosen = jnp.take_along_axis(label_order, position, axis=1)
    id_grid = chosen.reshape(blocks, TOPK, TOK_DEV).transpose(0, 2, 1)
    row_keys = jax.random.split(row_key, blocks)
    sorted_row_index = jax.vmap(lambda sub_key: jax.random.permutation(sub_key, TOK_DEV))(row_keys)
    id_grid = jnp.take_along_axis(id_grid, sorted_row_index[:, :, None], axis=1)
    return id_grid.reshape(LAYERS, MB, N_EXPERT * TOK_DEV, TOPK).astype(jnp.int32)


def steps_of(stream_key, shape, cuts, low, top_value):
    loudness, own = 1.0, jax.random.fold_in(stream_key, 6)
    for axis_at, parts in cuts:
        heights = jnp.exp(jax.random.uniform(jax.random.fold_in(own, axis_at), (parts,), jnp.float32, low / len(cuts), top_value / len(cuts)))
        loudness = loudness * jnp.repeat(heights, shape[axis_at] // parts).reshape([-1 if axis == axis_at else 1 for axis in range(len(shape))])
    return loudness


def scatter_about(rng, dims, scale, most, shards=(), held_as=jnp.bfloat16):
    entries = jax.random.normal(rng, dims, jnp.float32) * scale
    if len(shards) > 0:
        entries = steps_of(rng, dims, shards, -0.22, 0.18) * entries
    return jnp.clip(entries, min=-most, max=most).astype(held_as)


def setup_inputs(seed: int = 0) -> dict:
    arg_keys = jax.random.split(jax.random.key(seed), 7)
    tokens_in = scatter_about(arg_keys[0], (MB, TOKENS, D), 1.0, 6.0, ((1, 32),))
    expert_ids = draw_expert_ids(jax.random.fold_in(arg_keys[6], 71), 0)
    gate_values = jnp.clip(jnp.exp(math.log(1.0) - 2.3025851 * jax.random.uniform(arg_keys[2], (LAYERS, MB, TOKENS, TOPK), jnp.float32) ** steps_of(arg_keys[2], (LAYERS, MB, TOKENS, TOPK), ((0, 8), (2, 32)), -0.2, 0.2)), 0.1, 1.0)
    expert_gate = scatter_about(arg_keys[3], (LAYERS, EXPERT_TOTAL, D, FF), D ** -0.5, 0.125, ((0, 8), (1, 32)))
    expert_up = scatter_about(arg_keys[4], (LAYERS, EXPERT_TOTAL, D, FF), D ** -0.5, 0.125, ((0, 8), (1, 32)))
    expert_down = scatter_about(arg_keys[5], (LAYERS, EXPERT_TOTAL, FF, D), FF ** -0.5, 0.21875, ((0, 8), (1, 32)))
    return {"tokens_in": tokens_in, "expert_ids": expert_ids, "gate_values": gate_values, "expert_gate": expert_gate, "expert_up": expert_up, "expert_down": expert_down}


epsilon = 1e-06

def apply_expert(operands):
    row_block, gate_matrix, up_matrix, down_matrix = operands
    widened_rows = row_block.astype(jnp.float32)
    gate_part = jnp.dot(widened_rows, gate_matrix.astype(jnp.float32), preferred_element_type=jnp.float32)
    up_part = jnp.dot(widened_rows, up_matrix.astype(jnp.float32), preferred_element_type=jnp.float32)
    activated = (jax.nn.silu(gate_part) * up_part).astype(jnp.bfloat16)
    return jnp.dot(activated.astype(jnp.float32), down_matrix.astype(jnp.float32), preferred_element_type=jnp.float32).astype(jnp.bfloat16)

def expert_layer(hidden, route_ids, gate_rows, stacked_gate_weights, up_stack, down_stack):
    widened = hidden.reshape(MB * TOKENS, D).astype(jnp.float32)
    normed = (widened * lax.rsqrt(lax.optimization_barrier(jnp.mean(widened * widened, axis=-1, keepdims=True)) + epsilon)).astype(jnp.bfloat16)
    slot_capacity = MB * N_EXPERT * MOST
    flat_ids = route_ids.reshape(MB * TOKENS * TOPK).astype(jnp.int32)
    onehot = (flat_ids[:, None] == jnp.arange(EXPERT_TOTAL, dtype=jnp.int32)[None, :]).astype(jnp.int32)
    ahead_count = (jnp.cumsum(onehot, axis=0) - onehot).astype(jnp.int32)
    place_in = lax.optimization_barrier(jnp.sum(ahead_count * onehot, axis=1)).astype(jnp.int32)
    target = (flat_ids * slot_capacity + place_in).astype(jnp.int32)
    owner_row = (jnp.arange(MB * TOKENS * TOPK, dtype=jnp.int32) // TOPK).astype(jnp.int32)
    source = jnp.full((EXPERT_TOTAL * slot_capacity,), MB * TOKENS, jnp.int32).at[target].set(owner_row)
    padded = jnp.concatenate([normed, jnp.zeros((1, D), jnp.bfloat16)], axis=0)
    grouped = padded[source].reshape(EXPERT_TOTAL, slot_capacity, D)
    results = lax.map(apply_expert, (grouped, stacked_gate_weights, up_stack, down_stack)).reshape(EXPERT_TOTAL * slot_capacity, D)
    picked = results[target].reshape(MB * TOKENS, TOPK, D).astype(jnp.float32)
    weights_flat = gate_rows.reshape(MB * TOKENS, TOPK).astype(jnp.float32)
    combined = widened + lax.optimization_barrier(jnp.sum(weights_flat[:, :, None] * picked, axis=1))
    return combined.astype(jnp.bfloat16).reshape(MB, TOKENS, D)

def reference(tokens_in, expert_ids, gate_values, expert_gate, expert_up, expert_down):
    collected = []
    hidden = tokens_in
    for layer_index in range(LAYERS):
        hidden = expert_layer(hidden, expert_ids[layer_index], gate_values[layer_index], expert_gate[layer_index], expert_up[layer_index], expert_down[layer_index])
        collected.append(hidden)
    return jnp.stack(collected)
```

```python
import jax
import jax.numpy as jnp
from jax import lax
from jax.experimental import pallas as pl
from jax.experimental.pallas import tpu as pltpu
from jax.sharding import PartitionSpec as P

epsilon = 1e-06
MESH = pl.DeviceIdType.MESH
STREAMS = 4
ORDER = (("spread", 0), ("expert", 3), ("finish", 6), ("combine", 4), ("route", 1))
most_rows = 6


def make_kernel(sizes, streams, order):
    nsec, nx, nz, batches, tok, topk, feat, ff, slot = sizes
    src_count = nz // streams
    width = src_count * tok
    items = batches * streams
    rows = nx * slot

    def kernel(
        tok_ref, ids_ref, gate_ref, wg_hbm, wu_hbm, wd_hbm, out_ref,
        wg, wu, wd, hbuf, ag, sel, xs, xr, hid, ys, yr, ps, zr, gbuf,
        w_sem, h_sem, hs_sem, g_sem, gs_sem,
        z1_sem, z1s_sem, x1_sem, x1s_sem, x2_sem, x2s_sem, z2_sem, z2s_sem,
    ):
        sec = lax.axis_index("section")
        me = lax.axis_index("expert")
        x = me // nz
        z = me % nz
        my_q = z % streams
        my_i = z // streams

        def dev(xx, zz):
            return (sec, xx * nz + zz)

        def remote(src, dst, ssem, rsem, where):
            return pltpu.make_async_remote_copy(
                src_ref=src, dst_ref=dst, send_sem=ssem, recv_sem=rsem,
                device_id=where, device_id_type=MESH,
            )

        z_peers = [(z + d) % nz for d in (4, 3, 5, 2, 6, 1, 7)]
        x_peers = [(x + d) % nx for d in (2, 1, 3)]
        following = (lax.rem(sec + 1, nsec), me)
        preceding = (lax.rem(sec + nsec - 1, nsec), me)
        everyone = [dev(x, zz) for zz in z_peers] + [dev(xx, z) for xx in x_peers]
        everyone += [following, preceding]
        barrier = pltpu.get_barrier_semaphore()

        weights = [
            pltpu.make_async_copy(a, b, w_sem.at[k])
            for k, (a, b) in enumerate(((wg_hbm, wg), (wu_hbm, wu), (wd_hbm, wd)))
        ]
        first = pltpu.make_async_copy(tok_ref, hbuf, h_sem.at[batches])

        @pl.when(sec == 0)
        def _():
            first.start()

        for copy in weights:
            copy.start()
        for peer in everyone:
            pl.semaphore_signal(barrier, inc=1, device_id=peer, device_id_type=MESH)
        gbuf[z] = gate_ref[...]
        pl.semaphore_wait(barrier, len(everyone))

        @pl.when(sec == 0)
        def _():
            first.wait()

        def split(j):
            return lax.div(j, streams), lax.rem(j, streams)

        def block(i):
            return pl.ds(pl.multiple_of(i * tok, tok), tok)

        def slots(i):
            return pl.ds(pl.multiple_of(i * slot, 8), slot)

        def spread(j):
            m, q = split(j)

            @pl.when(q == my_q)
            def _():
                @pl.when(sec > 0)
                def _():
                    remote(out_ref.at[m], hbuf.at[m], hs_sem.at[m], h_sem.at[m], following).wait_recv()

                widened = hbuf[m].astype(jnp.float32)
                inverse = lax.rsqrt(jnp.mean(widened * widened, axis=-1, keepdims=True) + epsilon)
                ag[j, block(my_i), :] = (widened * inverse).astype(jnp.bfloat16)
                mine = ag.at[j, block(my_i)]
                for zz in z_peers:
                    remote(mine, mine, z1s_sem.at[j], z1_sem.at[j], dev(x, zz)).start()

            @pl.when(j == 0)
            def _():
                for zz in z_peers:
                    remote(gbuf.at[z], gbuf.at[z], gs_sem, g_sem, dev(x, zz)).start()

        def wait_blocks(j, q, sem, buf, own):
            count = src_count - own

            @pl.when((q == my_q) if own else (q != my_q))
            def _():
                part = buf.at[j, pl.ds(0, count * tok)]
                remote(part, part, sem.at[j], sem.at[j], following).wait_recv()

        def route(j):
            m, q = split(j)
            for own in (0, 1):
                if own < src_count and (own == 1 or streams > 1):
                    wait_blocks(j, q, z1_sem, ag, own)
            ids = ids_ref[j]
            picked = [jnp.where(ids == xx * nz + z, 1.0, 0.0).astype(jnp.float32) for xx in range(nx)]
            masks = jnp.concatenate(picked, axis=0)
            r_id = lax.broadcasted_iota(jnp.int32, (width, width), 0)
            c_id = lax.broadcasted_iota(jnp.int32, (width, width), 1)
            earlier = jnp.where(r_id < c_id, 1.0, 0.0).astype(jnp.bfloat16)
            ahead = jnp.dot(masks.astype(jnp.bfloat16), earlier, preferred_element_type=jnp.float32)
            slot_id = lax.broadcasted_iota(jnp.int32, (slot, width), 0).astype(jnp.float32)
            parts = []
            for xx in range(nx):
                named = jnp.sum(picked[xx], axis=0, keepdims=True)
                rank = jnp.sum(ahead[topk * xx : topk * xx + topk], axis=0, keepdims=True)
                parts.append(jnp.where(slot_id == rank, named, 0.0))
            chosen = jnp.concatenate(parts, axis=0).astype(jnp.bfloat16)
            sel[j] = chosen
            xs[j] = jnp.dot(chosen, ag[j], preferred_element_type=jnp.float32).astype(jnp.bfloat16)
            for xx in x_peers:
                remote(
                    xs.at[j, slots(xx)], xr.at[j, slots(x)], x1s_sem.at[j], x1_sem.at[j], dev(xx, z)
                ).start()
            xr[j, slots(x), :] = xs[j, slots(x), :]

        def expert(j):
            part = xr.at[j, pl.ds(0, (nx - 1) * slot)]
            remote(part, part, x1s_sem.at[j], x1_sem.at[j], following).wait_recv()

            @pl.when(j == 0)
            def _():
                for copy in weights:
                    copy.wait()

            gate = jnp.dot(xr[j], wg[...], preferred_element_type=jnp.float32)
            up = jnp.dot(xr[j], wu[...], preferred_element_type=jnp.float32)
            hid[...] = (gate / (1.0 + jnp.exp(-gate)) * up).astype(jnp.bfloat16)
            ys[j] = jnp.dot(hid[...], wd[...], preferred_element_type=jnp.float32).astype(jnp.bfloat16)
            for xx in x_peers:
                remote(
                    ys.at[j, slots(xx)], yr.at[j, slots(x)], x2s_sem.at[j], x2_sem.at[j], dev(xx, z)
                ).start()
            yr[j, slots(x), :] = ys[j, slots(x), :]

        def combine(j):
            m, q = split(j)

            @pl.when(j == 0)
            def _():
                part = gbuf.at[pl.ds(0, nz - 1)]
                remote(part, part, gs_sem, g_sem, following).wait_recv()

            part = yr.at[j, pl.ds(0, (nx - 1) * slot)]
            remote(part, part, x2s_sem.at[j], x2_sem.at[j], following).wait_recv()
            ids = ids_ref[j]
            gates = gbuf[q, m]
            for i in range(1, src_count):
                gates = gates + gbuf[i * streams + q, m]
            high, low = [], []
            for xx in range(nx):
                weight = jnp.sum(jnp.where(ids == xx * nz + z, gates, 0.0), axis=0, keepdims=True)
                top = weight.astype(jnp.bfloat16).astype(jnp.float32)
                high.append(jnp.broadcast_to(top, (slot, width)))
                low.append(jnp.broadcast_to(weight - top, (slot, width)))
            chosen = sel[j].astype(jnp.float32)
            high = (chosen * jnp.concatenate(high, axis=0)).astype(jnp.bfloat16)
            low = (chosen * jnp.concatenate(low, axis=0)).astype(jnp.bfloat16)
            dims = (((0,), (0,)), ((), ()))
            total = lax.dot_general(high, yr[j], dims, preferred_element_type=jnp.float32)
            total = total + lax.dot_general(low, yr[j], dims, preferred_element_type=jnp.float32)
            ps[j] = total.astype(jnp.bfloat16)
            for i in range(src_count):
                target = i * streams + q

                @pl.when(target != z)
                def _():
                    remote(
                        ps.at[j, pl.ds(i * tok, tok)], zr.at[m, block(z)],
                        z2s_sem.at[j], z2_sem.at[m], dev(x, target),
                    ).start()

                @pl.when(target == z)
                def _():
                    zr[m, block(z), :] = ps[j, pl.ds(i * tok, tok), :]

        def finish(j):
            m, q = split(j)

            @pl.when(q == my_q)
            def _():
                part = zr.at[m, pl.ds(0, (nz - 1) * tok)]
                remote(part, part, z2_sem.at[m], z2_sem.at[m], following).wait_recv()
                total = zr[m, pl.ds(0, tok), :].astype(jnp.float32)
                for i in range(1, nz):
                    total = total + zr[m, pl.ds(i * tok, tok), :].astype(jnp.float32)
                out_ref[m] = (hbuf[m].astype(jnp.float32) + total).astype(jnp.bfloat16)

                @pl.when(sec < nsec - 1)
                def _():
                    remote(out_ref.at[m], hbuf.at[m], hs_sem.at[m], h_sem.at[m], following).start()

        stages = dict(spread=spread, route=route, expert=expert, combine=combine, finish=finish)
        last_lag = max(lag for _, lag in order)

        def one_step(i, carry):
            for name, lag in order:

                @pl.when((i >= lag) & (i < items + lag))
                def _():
                    stages[name](i - lag)

            return carry

        lax.fori_loop(0, items + last_lag, one_step, 0)

        def drain(j, carry):
            m, q = split(j)
            three = xs.at[j, pl.ds(0, (nx - 1) * slot)]
            remote(three, three, x1s_sem.at[j], x1_sem.at[j], following).wait_send()
            remote(three, three, x2s_sem.at[j], x2_sem.at[j], following).wait_send()
            few = ag.at[j, pl.ds(0, (src_count - 1) * tok)]
            many = ag.at[j]

            @pl.when(q == my_q)
            def _():
                seven = zr.at[m, pl.ds(0, (nz - 1) * tok)]
                remote(seven, seven, z1s_sem.at[j], z1_sem.at[j], following).wait_send()
                if src_count > 1:
                    remote(few, few, z2s_sem.at[j], z2_sem.at[m], following).wait_send()

                @pl.when(sec < nsec - 1)
                def _():
                    remote(out_ref.at[m], hbuf.at[m], hs_sem.at[m], h_sem.at[m], following).wait_send()

            @pl.when(q != my_q)
            def _():
                remote(many, many, z2s_sem.at[j], z2_sem.at[m], following).wait_send()

            return carry

        lax.fori_loop(0, items, drain, 0)
        seven = gbuf.at[pl.ds(0, nz - 1)]
        remote(seven, seven, gs_sem, g_sem, following).wait_send()

    bf16 = jnp.bfloat16
    dma = pltpu.SemaphoreType.DMA
    scratch = [
        pltpu.VMEM((feat, ff), bf16), pltpu.VMEM((feat, ff), bf16), pltpu.VMEM((ff, feat), bf16),
        pltpu.VMEM((batches, tok, feat), bf16),
        pltpu.VMEM((items, width, feat), bf16),
        pltpu.VMEM((items, rows, width), bf16),
        pltpu.VMEM((items, rows, feat), bf16), pltpu.VMEM((items, rows, feat), bf16),
        pltpu.VMEM((rows, ff), bf16),
        pltpu.VMEM((items, rows, feat), bf16), pltpu.VMEM((items, rows, feat), bf16),
        pltpu.VMEM((items, width, feat), bf16),
        pltpu.VMEM((batches, nz * tok, feat), bf16),
        pltpu.VMEM((nz, batches, topk, width), jnp.float32),
        dma((3,)), dma((batches + 1,)), dma((batches,)), dma, dma,
        dma((items,)), dma((items,)), dma((items,)), dma((items,)),
        dma((items,)), dma((items,)), dma((batches,)), dma((items,)),
    ]
    return kernel, scratch


def solution(mesh, streams=STREAMS, order=ORDER):
    nsec = mesh.shape["section"]
    nx, nz = 4, mesh.shape["expert"] // 4

    def body(tokens_in, expert_ids, gate_values, expert_gate, expert_up, expert_down):
        batches, tok, feat = tokens_in.shape
        topk = expert_ids.shape[3]
        ff = expert_gate.shape[3]
        src_count = nz // streams
        width = src_count * tok
        items = batches * streams
        slot = -(-src_count * most_rows // 8) * 8
        me = lax.axis_index("expert")
        ids = lax.dynamic_slice_in_dim(expert_ids[0], (me // nz) * (nz * tok), nz * tok, 1)
        ids = ids.reshape(batches, src_count, streams, tok, topk)
        ids = ids.transpose(0, 2, 4, 1, 3).reshape(items, topk, width)
        gates = jnp.swapaxes(gate_values[0], 1, 2)
        lanes = jnp.arange(width, dtype=jnp.int32) // tok
        gates = jnp.where(lanes == (me % nz) // streams, jnp.tile(gates, (1, 1, src_count)), 0.0)
        sizes = (nsec, nx, nz, batches, tok, topk, feat, ff, slot)
        kernel, scratch = make_kernel(sizes, streams, order)
        vmem = pl.BlockSpec(memory_space=pltpu.VMEM)
        hbm = pl.BlockSpec(memory_space=pl.ANY)
        out = pl.pallas_call(
            kernel,
            out_shape=jax.ShapeDtypeStruct((batches, tok, feat), jnp.bfloat16),
            in_specs=[hbm, vmem, vmem, hbm, hbm, hbm],
            out_specs=vmem,
            scratch_shapes=scratch,
            compiler_params=pltpu.CompilerParams(
                collective_id=0, has_side_effects=True, vmem_limit_bytes=67000000
            ),
            name="relay",
        )(tokens_in, ids, gates, expert_gate[0, 0], expert_up[0, 0], expert_down[0, 0])
        return out[None]

    return jax.shard_map(
        body,
        mesh=mesh,
        in_specs=(
            P(None, "expert", None),
            P("section", None, None, None),
            P("section", None, "expert", None),
            P("section", "expert", None, None),
            P("section", "expert", None, None),
            P("section", "expert", None, None),
        ),
        out_specs=P("section", None, "expert", None),
        check_vma=False,
    )
```

```python
import jax
import jax.numpy as jnp
from jax import lax
from jax.experimental import pallas as pl
from jax.experimental.pallas import tpu as pltpu
from jax.sharding import PartitionSpec as P

epsilon = 1e-06
MESH = pl.DeviceIdType.MESH
STREAMS = 4
ORDER = (("spread", 0), ("expert", 3), ("combine", 4), ("route", 1))
most_rows = 6


def make_kernel(sizes, streams, order):
    nsec, nx, nz, batches, tok, topk, feat, ff, slot = sizes
    src_count = nz // streams
    width = src_count * tok
    items = batches * streams
    rows = nx * slot

    def kernel(
        tok_ref, ids_ref, gate_ref, wg_hbm, wu_hbm, wd_hbm, out_ref,
        wg, wu, wd, hbuf, rbuf, ag, sel, xs, xr, hid, ys, yr, ps, zr, gbuf,
        w_sem, h_sem, hs_sem, o_sem, os_sem, g_sem, gs_sem,
        z1_sem, z1s_sem, x1_sem, x1s_sem, x2_sem, x2s_sem, z2_sem, z2s_sem,
    ):
        sec = lax.axis_index("section")
        me = lax.axis_index("expert")
        x = me // nz
        z = me % nz
        my_q = z % streams
        my_i = z // streams

        def dev(xx, zz):
            return (sec, xx * nz + zz)

        def remote(src, dst, ssem, rsem, where):
            return pltpu.make_async_remote_copy(
                src_ref=src, dst_ref=dst, send_sem=ssem, recv_sem=rsem,
                device_id=where, device_id_type=MESH,
            )

        z_peers = [(z + d) % nz for d in (4, 3, 5, 2, 6, 1, 7)]
        x_peers = [(x + d) % nx for d in (2, 1, 3)]
        following = (lax.rem(sec + 1, nsec), me)
        preceding = (lax.rem(sec + nsec - 1, nsec), me)
        everyone = [dev(x, zz) for zz in z_peers] + [dev(xx, z) for xx in x_peers]
        after, before = following[0], preceding[0]
        everyone += [(ss, x * nz + zz) for ss in (after, before) for zz in range(nz)]
        barrier = pltpu.get_barrier_semaphore()

        weights = [
            pltpu.make_async_copy(a, b, w_sem.at[k])
            for k, (a, b) in enumerate(((wg_hbm, wg), (wu_hbm, wu), (wd_hbm, wd)))
        ]
        first = pltpu.make_async_copy(tok_ref, hbuf, h_sem.at[batches])

        @pl.when(sec == 0)
        def _():
            first.start()

        for copy in weights:
            copy.start()
        for peer in everyone:
            pl.semaphore_signal(barrier, inc=1, device_id=peer, device_id_type=MESH)
        gbuf[z] = gate_ref[...]
        pl.semaphore_wait(barrier, len(everyone))

        @pl.when(sec == 0)
        def _():
            first.wait()

        def split(j):
            return lax.div(j, streams), lax.rem(j, streams)

        def block(i):
            return pl.ds(pl.multiple_of(i * tok, tok), tok)

        def slots(i):
            return pl.ds(pl.multiple_of(i * slot, 8), slot)

        def absorb(m):
            remote(rbuf.at[m], rbuf.at[m], hs_sem.at[m], h_sem.at[m], following).wait_recv()
            remote(zr.at[m], zr.at[m], z2_sem.at[m], z2_sem.at[m], following).wait_recv()
            total = zr[m, pl.ds(0, tok), :].astype(jnp.float32)
            for i in range(1, nz):
                total = total + zr[m, pl.ds(i * tok, tok), :].astype(jnp.float32)
            hbuf[m] = (rbuf[m].astype(jnp.float32) + total).astype(jnp.bfloat16)

        def hand_back(m):
            return remote(hbuf.at[m], out_ref.at[m], os_sem.at[m], o_sem.at[m], preceding)

        def hand_on(m):
            return remote(hbuf.at[m], rbuf.at[m], hs_sem.at[m], h_sem.at[m], following)

        def spread(j):
            m, q = split(j)

            @pl.when(q == my_q)
            def _():
                @pl.when(sec > 0)
                def _():
                    absorb(m)

                widened = hbuf[m].astype(jnp.float32)
                inverse = lax.rsqrt(jnp.mean(widened * widened, axis=-1, keepdims=True) + epsilon)
                ag[j, block(my_i), :] = (widened * inverse).astype(jnp.bfloat16)
                mine = ag.at[j, block(my_i)]
                for zz in z_peers:
                    remote(mine, mine, z1s_sem.at[j], z1_sem.at[j], dev(x, zz)).start()
                hand_on(m).start()

                @pl.when(sec > 0)
                def _():
                    hand_back(m).start()

            @pl.when(j == 0)
            def _():
                for zz in z_peers:
                    remote(gbuf.at[z], gbuf.at[z], gs_sem, g_sem, dev(x, zz)).start()

        def wait_blocks(j, q, sem, buf, own):
            count = src_count - own

            @pl.when((q == my_q) if own else (q != my_q))
            def _():
                part = buf.at[j, pl.ds(0, count * tok)]
                remote(part, part, sem.at[j], sem.at[j], following).wait_recv()

        def route(j):
            m, q = split(j)
            for own in (0, 1):
                if own < src_count and (own == 1 or streams > 1):
                    wait_blocks(j, q, z1_sem, ag, own)
            ids = ids_ref[j]
            picked = [jnp.where(ids == xx * nz + z, 1.0, 0.0).astype(jnp.float32) for xx in range(nx)]
            masks = jnp.concatenate(picked, axis=0)
            r_id = lax.broadcasted_iota(jnp.int32, (width, width), 0)
            c_id = lax.broadcasted_iota(jnp.int32, (width, width), 1)
            earlier = jnp.where(r_id < c_id, 1.0, 0.0).astype(jnp.bfloat16)
            ahead = jnp.dot(masks.astype(jnp.bfloat16), earlier, preferred_element_type=jnp.float32)
            slot_id = lax.broadcasted_iota(jnp.int32, (slot, width), 0).astype(jnp.float32)
            parts = []
            for xx in range(nx):
                named = jnp.sum(picked[xx], axis=0, keepdims=True)
                rank = jnp.sum(ahead[topk * xx : topk * xx + topk], axis=0, keepdims=True)
                parts.append(jnp.where(slot_id == rank, named, 0.0))
            chosen = jnp.concatenate(parts, axis=0).astype(jnp.bfloat16)
            sel[j] = chosen
            xs[j] = jnp.dot(chosen, ag[j], preferred_element_type=jnp.float32).astype(jnp.bfloat16)
            for xx in x_peers:
                remote(
                    xs.at[j, slots(xx)], xr.at[j, slots(x)], x1s_sem.at[j], x1_sem.at[j], dev(xx, z)
                ).start()
            xr[j, slots(x), :] = xs[j, slots(x), :]

        def expert(j):
            part = xr.at[j, pl.ds(0, (nx - 1) * slot)]
            remote(part, part, x1s_sem.at[j], x1_sem.at[j], following).wait_recv()

            @pl.when(j == 0)
            def _():
                for copy in weights:
                    copy.wait()

            gate = jnp.dot(xr[j], wg[...], preferred_element_type=jnp.float32)
            up = jnp.dot(xr[j], wu[...], preferred_element_type=jnp.float32)
            hid[...] = (gate / (1.0 + jnp.exp(-gate)) * up).astype(jnp.bfloat16)
            ys[j] = jnp.dot(hid[...], wd[...], preferred_element_type=jnp.float32).astype(jnp.bfloat16)
            for xx in x_peers:
                remote(
                    ys.at[j, slots(xx)], yr.at[j, slots(x)], x2s_sem.at[j], x2_sem.at[j], dev(xx, z)
                ).start()
            yr[j, slots(x), :] = ys[j, slots(x), :]

        def combine(j):
            m, q = split(j)

            @pl.when(j == 0)
            def _():
                part = gbuf.at[pl.ds(0, nz - 1)]
                remote(part, part, gs_sem, g_sem, following).wait_recv()

            part = yr.at[j, pl.ds(0, (nx - 1) * slot)]
            remote(part, part, x2s_sem.at[j], x2_sem.at[j], following).wait_recv()
            ids = ids_ref[j]
            gates = gbuf[q, m]
            for i in range(1, src_count):
                gates = gates + gbuf[i * streams + q, m]
            high, low = [], []
            for xx in range(nx):
                weight = jnp.sum(jnp.where(ids == xx * nz + z, gates, 0.0), axis=0, keepdims=True)
                top = weight.astype(jnp.bfloat16).astype(jnp.float32)
                high.append(jnp.broadcast_to(top, (slot, width)))
                low.append(jnp.broadcast_to(weight - top, (slot, width)))
            chosen = sel[j].astype(jnp.float32)
            high = (chosen * jnp.concatenate(high, axis=0)).astype(jnp.bfloat16)
            low = (chosen * jnp.concatenate(low, axis=0)).astype(jnp.bfloat16)
            dims = (((0,), (0,)), ((), ()))
            total = lax.dot_general(high, yr[j], dims, preferred_element_type=jnp.float32)
            total = total + lax.dot_general(low, yr[j], dims, preferred_element_type=jnp.float32)
            ps[j] = total.astype(jnp.bfloat16)
            for i in range(src_count):
                target = x * nz + i * streams + q
                remote(
                    ps.at[j, pl.ds(i * tok, tok)], zr.at[m, block(z)],
                    z2s_sem.at[j], z2_sem.at[m], (after, target),
                ).start()

        stages = dict(spread=spread, route=route, expert=expert, combine=combine)
        last_lag = max(lag for _, lag in order)

        def one_step(i, carry):
            for name, lag in order:

                @pl.when((i >= lag) & (i < items + lag))
                def _():
                    stages[name](i - lag)

            return carry

        lax.fori_loop(0, items + last_lag, one_step, 0)

        def drain(j, carry):
            m, q = split(j)
            three = xs.at[j, pl.ds(0, (nx - 1) * slot)]
            remote(three, three, x1s_sem.at[j], x1_sem.at[j], following).wait_send()
            remote(three, three, x2s_sem.at[j], x2_sem.at[j], following).wait_send()
            many = ag.at[j]
            remote(many, many, z2s_sem.at[j], z2_sem.at[m], following).wait_send()

            @pl.when(q == my_q)
            def _():
                seven = zr.at[m, pl.ds(0, (nz - 1) * tok)]
                remote(seven, seven, z1s_sem.at[j], z1_sem.at[j], following).wait_send()
                hand_on(m).wait_send()

                @pl.when(sec > 0)
                def _():
                    hand_back(m).wait_send()

            return carry

        lax.fori_loop(0, items, drain, 0)
        seven = gbuf.at[pl.ds(0, nz - 1)]
        remote(seven, seven, gs_sem, g_sem, following).wait_send()

        @pl.when(sec == 0)
        def _():
            def close(m, carry):
                absorb(m)
                hand_back(m).start()
                return carry

            def closed(m, carry):
                hand_back(m).wait_send()
                return carry

            lax.fori_loop(0, batches, close, 0)
            lax.fori_loop(0, batches, closed, 0)

        def arrived(m, carry):
            hand_back(m).wait_recv()
            return carry

        lax.fori_loop(0, batches, arrived, 0)

    bf16 = jnp.bfloat16
    dma = pltpu.SemaphoreType.DMA
    scratch = [
        pltpu.VMEM((feat, ff), bf16), pltpu.VMEM((feat, ff), bf16), pltpu.VMEM((ff, feat), bf16),
        pltpu.VMEM((batches, tok, feat), bf16), pltpu.VMEM((batches, tok, feat), bf16),
        pltpu.VMEM((items, width, feat), bf16),
        pltpu.VMEM((items, rows, width), bf16),
        pltpu.VMEM((items, rows, feat), bf16), pltpu.VMEM((items, rows, feat), bf16),
        pltpu.VMEM((rows, ff), bf16),
        pltpu.VMEM((items, rows, feat), bf16), pltpu.VMEM((items, rows, feat), bf16),
        pltpu.VMEM((items, width, feat), bf16),
        pltpu.VMEM((batches, nz * tok, feat), bf16),
        pltpu.VMEM((nz, batches, topk, width), jnp.float32),
        dma((3,)), dma((batches + 1,)), dma((batches,)), dma((batches,)), dma((batches,)), dma, dma,
        dma((items,)), dma((items,)), dma((items,)), dma((items,)),
        dma((items,)), dma((items,)), dma((batches,)), dma((items,)),
    ]
    return kernel, scratch


def solution(mesh, streams=STREAMS, order=ORDER):
    nsec = mesh.shape["section"]
    nx, nz = 4, mesh.shape["expert"] // 4

    def body(tokens_in, expert_ids, gate_values, expert_gate, expert_up, expert_down):
        batches, tok, feat = tokens_in.shape
        topk = expert_ids.shape[3]
        ff = expert_gate.shape[3]
        src_count = nz // streams
        width = src_count * tok
        items = batches * streams
        slot = -(-src_count * most_rows // 8) * 8
        me = lax.axis_index("expert")
        ids = lax.dynamic_slice_in_dim(expert_ids[0], (me // nz) * (nz * tok), nz * tok, 1)
        ids = ids.reshape(batches, src_count, streams, tok, topk)
        ids = ids.transpose(0, 2, 4, 1, 3).reshape(items, topk, width)
        gates = jnp.swapaxes(gate_values[0], 1, 2)
        lanes = jnp.arange(width, dtype=jnp.int32) // tok
        gates = jnp.where(lanes == (me % nz) // streams, jnp.tile(gates, (1, 1, src_count)), 0.0)
        sizes = (nsec, nx, nz, batches, tok, topk, feat, ff, slot)
        kernel, scratch = make_kernel(sizes, streams, order)
        vmem = pl.BlockSpec(memory_space=pltpu.VMEM)
        hbm = pl.BlockSpec(memory_space=pl.ANY)
        out = pl.pallas_call(
            kernel,
            out_shape=jax.ShapeDtypeStruct((batches, tok, feat), jnp.bfloat16),
            in_specs=[hbm, vmem, vmem, hbm, hbm, hbm],
            out_specs=vmem,
            scratch_shapes=scratch,
            compiler_params=pltpu.CompilerParams(
                collective_id=0, has_side_effects=True, vmem_limit_bytes=67000000
            ),
            name="relay",
        )(tokens_in, ids, gates, expert_gate[0, 0], expert_up[0, 0], expert_down[0, 0])
        return out[None]

    return jax.shard_map(
        body,
        mesh=mesh,
        in_specs=(
            P(None, "expert", None),
            P("section", None, None, None),
            P("section", None, "expert", None),
            P("section", "expert", None, None),
            P("section", "expert", None, None),
            P("section", "expert", None, None),
        ),
        out_specs=P("section", None, "expert", None),
        check_vma=False,
    )
```

```python
import jax
import jax.numpy as jnp
from jax import lax
from jax.experimental import pallas as pl
from jax.experimental.pallas import tpu as pltpu
from jax.sharding import PartitionSpec as P

epsilon = 1e-06
MESH = pl.DeviceIdType.MESH
STREAMS = 4
ORDER = (("spread", 0), ("expert", 3), ("combine", 4), ("route", 1))
most_rows = 6


def make_kernel(sizes, streams, order):
    nsec, nx, nz, batches, tok, topk, feat, ff, slot = sizes
    src_count = nz // streams
    width = src_count * tok
    items = batches * streams
    rows = nx * slot

    def kernel(
        tok_ref, ids_ref, gate_ref, wg_hbm, wu_hbm, wd_hbm, out_ref,
        wg, wu, wd, hbuf, rbuf, ag, sel, xs, xr, hid, ys, yr, ps, zr, gbuf,
        w_sem, h_sem, hs_sem, o_sem, os_sem, g_sem, gs_sem,
        z1_sem, z1s_sem, x1_sem, x1s_sem, x2_sem, x2s_sem, z2_sem, z2s_sem,
    ):
        sec = lax.axis_index("section")
        me = lax.axis_index("expert")
        x = me // nz
        z = me % nz
        my_q = z % streams
        my_i = z // streams

        def dev(xx, zz):
            return (sec, xx * nz + zz)

        def remote(src, dst, ssem, rsem, where):
            return pltpu.make_async_remote_copy(
                src_ref=src, dst_ref=dst, send_sem=ssem, recv_sem=rsem,
                device_id=where, device_id_type=MESH,
            )

        z_peers = [(z + d) % nz for d in (4, 3, 5, 2, 6, 1, 7)]
        x_peers = [(x + d) % nx for d in (2, 1, 3)]
        following = (lax.rem(sec + 1, nsec), me)
        preceding = (lax.rem(sec + nsec - 1, nsec), me)
        everyone = [dev(x, zz) for zz in z_peers] + [dev(xx, z) for xx in x_peers]
        after, before = following[0], preceding[0]
        everyone += [(ss, x * nz + zz) for ss in (after, before) for zz in range(nz)]
        barrier = pltpu.get_barrier_semaphore()

        weights = [
            pltpu.make_async_copy(a, b, w_sem.at[k])
            for k, (a, b) in enumerate(((wg_hbm, wg), (wu_hbm, wu), (wd_hbm, wd)))
        ]
        first = pltpu.make_async_copy(tok_ref, hbuf, h_sem.at[batches])

        @pl.when(sec == 0)
        def _():
            first.start()

        for copy in weights:
            copy.start()
        for peer in everyone:
            pl.semaphore_signal(barrier, inc=1, device_id=peer, device_id_type=MESH)
        gbuf[z] = gate_ref[...]
        pl.semaphore_wait(barrier, len(everyone))

        @pl.when(sec == 0)
        def _():
            first.wait()

        def split(j):
            return lax.div(j, streams), lax.rem(j, streams)

        def block(i):
            return pl.ds(pl.multiple_of(i * tok, tok), tok)

        def slots(i):
            return pl.ds(pl.multiple_of(i * slot, 8), slot)

        def absorb(m):
            remote(rbuf.at[m], rbuf.at[m], hs_sem.at[m], h_sem.at[m], following).wait_recv()
            remote(zr.at[m], zr.at[m], z2_sem.at[m], z2_sem.at[m], following).wait_recv()
            total = zr[m, pl.ds(0, tok), :].astype(jnp.float32)
            for i in range(1, nz):
                total = total + zr[m, pl.ds(i * tok, tok), :].astype(jnp.float32)
            hbuf[m] = (rbuf[m].astype(jnp.float32) + total).astype(jnp.bfloat16)

        def hand_back(m):
            return remote(hbuf.at[m], out_ref.at[m], os_sem.at[m], o_sem.at[m], preceding)

        def hand_on(m):
            return remote(hbuf.at[m], rbuf.at[m], hs_sem.at[m], h_sem.at[m], following)

        def spread(j):
            m, q = split(j)

            @pl.when(q == my_q)
            def _():
                @pl.when(sec > 0)
                def _():
                    absorb(m)

                widened = hbuf[m].astype(jnp.float32)
                inverse = lax.rsqrt(jnp.mean(widened * widened, axis=-1, keepdims=True) + epsilon)
                ag[j, block(my_i), :] = (widened * inverse).astype(jnp.bfloat16)
                mine = ag.at[j, block(my_i)]
                for zz in z_peers:
                    remote(mine, mine, z1s_sem.at[j], z1_sem.at[j], dev(x, zz)).start()
                hand_on(m).start()

                @pl.when(sec > 0)
                def _():
                    hand_back(m).start()

            @pl.when(j == 0)
            def _():
                for zz in z_peers:
                    remote(gbuf.at[z], gbuf.at[z], gs_sem, g_sem, dev(x, zz)).start()

        def wait_blocks(j, q, sem, buf, own):
            count = src_count - own

            @pl.when((q == my_q) if own else (q != my_q))
            def _():
                part = buf.at[j, pl.ds(0, count * tok)]
                remote(part, part, sem.at[j], sem.at[j], following).wait_recv()

        def route(j):
            m, q = split(j)
            for own in (0, 1):
                if own < src_count and (own == 1 or streams > 1):
                    wait_blocks(j, q, z1_sem, ag, own)
            ids = ids_ref[j]
            picked = [jnp.where(ids == xx * nz + z, 1.0, 0.0).astype(jnp.float32) for xx in range(nx)]
            masks = jnp.concatenate(picked, axis=0)
            r_id = lax.broadcasted_iota(jnp.int32, (width, width), 0)
            c_id = lax.broadcasted_iota(jnp.int32, (width, width), 1)
            earlier = jnp.where(r_id < c_id, 1.0, 0.0).astype(jnp.bfloat16)
            ahead = jnp.dot(masks.astype(jnp.bfloat16), earlier, preferred_element_type=jnp.float32)
            slot_id = lax.broadcasted_iota(jnp.int32, (slot, width), 0).astype(jnp.float32)
            parts = []
            for xx in range(nx):
                named = jnp.sum(picked[xx], axis=0, keepdims=True)
                rank = jnp.sum(ahead[topk * xx : topk * xx + topk], axis=0, keepdims=True)
                parts.append(jnp.where(slot_id == rank, named, 0.0))
            chosen = jnp.concatenate(parts, axis=0).astype(jnp.bfloat16)
            sel[j] = chosen
            xs[j] = jnp.dot(chosen, ag[j], preferred_element_type=jnp.float32).astype(jnp.bfloat16)
            for xx in x_peers:
                remote(
                    xs.at[j, slots(xx)], xr.at[j, slots(x)], x1s_sem.at[j], x1_sem.at[j], dev(xx, z)
                ).start()
            xr[j, slots(x), :] = xs[j, slots(x), :]

        def expert(j):
            part = xr.at[j, pl.ds(0, (nx - 1) * slot)]
            remote(part, part, x1s_sem.at[j], x1_sem.at[j], following).wait_recv()

            @pl.when(j == 0)
            def _():
                for copy in weights:
                    copy.wait()

            gate = jnp.dot(xr[j], wg[...], preferred_element_type=jnp.float32)
            up = jnp.dot(xr[j], wu[...], preferred_element_type=jnp.float32)
            hid[...] = (gate / (1.0 + jnp.exp(-gate)) * up).astype(jnp.bfloat16)
            for first_col in (0, feat // 2):
                cols = pl.ds(first_col, feat // 2)
                ys[j, :, cols] = jnp.dot(
                    hid[...], wd[:, cols], preferred_element_type=jnp.float32
                ).astype(jnp.bfloat16)
                for xx in x_peers:
                    remote(
                        ys.at[j, slots(xx), cols], yr.at[j, slots(x), cols],
                        x2s_sem.at[j], x2_sem.at[j], dev(xx, z),
                    ).start()
            yr[j, slots(x), :] = ys[j, slots(x), :]

        def combine(j):
            m, q = split(j)

            @pl.when(j == 0)
            def _():
                part = gbuf.at[pl.ds(0, nz - 1)]
                remote(part, part, gs_sem, g_sem, following).wait_recv()

            part = yr.at[j, pl.ds(0, (nx - 1) * slot)]
            remote(part, part, x2s_sem.at[j], x2_sem.at[j], following).wait_recv()
            ids = ids_ref[j]
            gates = gbuf[q, m]
            for i in range(1, src_count):
                gates = gates + gbuf[i * streams + q, m]
            high, low = [], []
            for xx in range(nx):
                weight = jnp.sum(jnp.where(ids == xx * nz + z, gates, 0.0), axis=0, keepdims=True)
                top = weight.astype(jnp.bfloat16).astype(jnp.float32)
                high.append(jnp.broadcast_to(top, (slot, width)))
                low.append(jnp.broadcast_to(weight - top, (slot, width)))
            chosen = sel[j].astype(jnp.float32)
            high = (chosen * jnp.concatenate(high, axis=0)).astype(jnp.bfloat16)
            low = (chosen * jnp.concatenate(low, axis=0)).astype(jnp.bfloat16)
            dims = (((0,), (0,)), ((), ()))
            total = lax.dot_general(high, yr[j], dims, preferred_element_type=jnp.float32)
            total = total + lax.dot_general(low, yr[j], dims, preferred_element_type=jnp.float32)
            ps[j] = total.astype(jnp.bfloat16)
            for i in range(src_count):
                target = x * nz + i * streams + q
                remote(
                    ps.at[j, pl.ds(i * tok, tok)], zr.at[m, block(z)],
                    z2s_sem.at[j], z2_sem.at[m], (after, target),
                ).start()

        stages = dict(spread=spread, route=route, expert=expert, combine=combine)
        last_lag = max(lag for _, lag in order)

        def one_step(i, carry):
            for name, lag in order:

                @pl.when((i >= lag) & (i < items + lag))
                def _():
                    stages[name](i - lag)

            return carry

        lax.fori_loop(0, items + last_lag, one_step, 0)

        def drain(j, carry):
            m, q = split(j)
            three = xs.at[j, pl.ds(0, (nx - 1) * slot)]
            remote(three, three, x1s_sem.at[j], x1_sem.at[j], following).wait_send()
            remote(three, three, x2s_sem.at[j], x2_sem.at[j], following).wait_send()
            many = ag.at[j]
            remote(many, many, z2s_sem.at[j], z2_sem.at[m], following).wait_send()

            @pl.when(q == my_q)
            def _():
                seven = zr.at[m, pl.ds(0, (nz - 1) * tok)]
                remote(seven, seven, z1s_sem.at[j], z1_sem.at[j], following).wait_send()
                hand_on(m).wait_send()

                @pl.when(sec > 0)
                def _():
                    hand_back(m).wait_send()

            return carry

        lax.fori_loop(0, items, drain, 0)
        seven = gbuf.at[pl.ds(0, nz - 1)]
        remote(seven, seven, gs_sem, g_sem, following).wait_send()

        @pl.when(sec == 0)
        def _():
            def close(m, carry):
                absorb(m)
                hand_back(m).start()
                return carry

            def closed(m, carry):
                hand_back(m).wait_send()
                return carry

            lax.fori_loop(0, batches, close, 0)
            lax.fori_loop(0, batches, closed, 0)

        def arrived(m, carry):
            hand_back(m).wait_recv()
            return carry

        lax.fori_loop(0, batches, arrived, 0)

    bf16 = jnp.bfloat16
    dma = pltpu.SemaphoreType.DMA
    scratch = [
        pltpu.VMEM((feat, ff), bf16), pltpu.VMEM((feat, ff), bf16), pltpu.VMEM((ff, feat), bf16),
        pltpu.VMEM((batches, tok, feat), bf16), pltpu.VMEM((batches, tok, feat), bf16),
        pltpu.VMEM((items, width, feat), bf16),
        pltpu.VMEM((items, rows, width), bf16),
        pltpu.VMEM((items, rows, feat), bf16), pltpu.VMEM((items, rows, feat), bf16),
        pltpu.VMEM((rows, ff), bf16),
        pltpu.VMEM((items, rows, feat), bf16), pltpu.VMEM((items, rows, feat), bf16),
        pltpu.VMEM((items, width, feat), bf16),
        pltpu.VMEM((batches, nz * tok, feat), bf16),
        pltpu.VMEM((nz, batches, topk, width), jnp.float32),
        dma((3,)), dma((batches + 1,)), dma((batches,)), dma((batches,)), dma((batches,)), dma, dma,
        dma((items,)), dma((items,)), dma((items,)), dma((items,)),
        dma((items,)), dma((items,)), dma((batches,)), dma((items,)),
    ]
    return kernel, scratch


def solution(mesh, streams=STREAMS, order=ORDER):
    nsec = mesh.shape["section"]
    nx, nz = 4, mesh.shape["expert"] // 4

    def body(tokens_in, expert_ids, gate_values, expert_gate, expert_up, expert_down):
        batches, tok, feat = tokens_in.shape
        topk = expert_ids.shape[3]
        ff = expert_gate.shape[3]
        src_count = nz // streams
        width = src_count * tok
        items = batches * streams
        slot = -(-src_count * most_rows // 8) * 8
        me = lax.axis_index("expert")
        ids = lax.dynamic_slice_in_dim(expert_ids[0], (me // nz) * (nz * tok), nz * tok, 1)
        ids = ids.reshape(batches, src_count, streams, tok, topk)
        ids = ids.transpose(0, 2, 4, 1, 3).reshape(items, topk, width)
        gates = jnp.swapaxes(gate_values[0], 1, 2)
        lanes = jnp.arange(width, dtype=jnp.int32) // tok
        gates = jnp.where(lanes == (me % nz) // streams, jnp.tile(gates, (1, 1, src_count)), 0.0)
        sizes = (nsec, nx, nz, batches, tok, topk, feat, ff, slot)
        kernel, scratch = make_kernel(sizes, streams, order)
        vmem = pl.BlockSpec(memory_space=pltpu.VMEM)
        hbm = pl.BlockSpec(memory_space=pl.ANY)
        out = pl.pallas_call(
            kernel,
            out_shape=jax.ShapeDtypeStruct((batches, tok, feat), jnp.bfloat16),
            in_specs=[hbm, vmem, vmem, hbm, hbm, hbm],
            out_specs=vmem,
            scratch_shapes=scratch,
            compiler_params=pltpu.CompilerParams(
                collective_id=0, has_side_effects=True, vmem_limit_bytes=67000000
            ),
            name="relay",
        )(tokens_in, ids, gates, expert_gate[0, 0], expert_up[0, 0], expert_down[0, 0])
        return out[None]

    return jax.shard_map(
        body,
        mesh=mesh,
        in_specs=(
            P(None, "expert", None),
            P("section", None, None, None),
            P("section", None, "expert", None),
            P("section", "expert", None, None),
            P("section", "expert", None, None),
            P("section", "expert", None, None),
        ),
        out_specs=P("section", None, "expert", None),
        check_vma=False,
    )
```
